256 devices in a mesh: gx: 16 (over z, core), gy: 16 (over y, x).
Axes of the slice: x: 4, y: 4, z: 8, core: 2. Of those that a mesh axis runs over, the one named last changes fastest.
Arguments:
- modes: float32 [524288, 512], P(('gx', 'gy'))
- batch: float32 [524288, 256], P(('gx', 'gy')), as said below
- core: float32 [768, 512], replicated, may hold values from -0.21875 to 0.21875
Outputs:
- new_modes: float32 [524288, 512], P(('gx', 'gy'))
The draws below stay inside these ranges and needn't reach their ends.
Inputs may be any that keep to these rules, and one draw needn't show every extreme that they name: Each row of modes and batch shares one positive scale; batch holds a sizeable part of the span of modes.
All inputs are finite; a program needn't handle non-finite values.
Results may differ from the reference program's by a relative error of at most 0.000058.
Values sent between devices are 32-bit elements; how exact they have to be, the bound alone decides.
A program may use at most 64 MiB of HBM per device.

```python
import math
import jax
import jax.numpy as jnp
from jax import lax

K = 512
B = 256
KB = 768
ROWS = 524288


def common_fields(key):
    base = jax.random.normal(jax.random.fold_in(key, 11), (ROWS, K), jnp.float32)
    noise = jax.random.normal(jax.random.fold_in(key, 12), (ROWS, B), jnp.float32)
    scale = jnp.exp(jax.random.uniform(jax.random.fold_in(key, 13), (ROWS, 1), jnp.float32, -0.7, 0.7)) / math.sqrt(math.sinh(1.4) / 1.4)
    weight = jnp.exp(jax.random.uniform(jax.random.fold_in(key, 14), (1, B), jnp.float32, -1.2, 0.7))
    modes = base * scale
    batch = (weight * base[:, K - B:] + noise) * scale
    return (modes, batch)


def draw_modes(key, part):
    return common_fields(key)[0]


def draw_batch(key, part):
    return common_fields(key)[1]


def gaussian(own_key, shape, width, bound, dtype=jnp.bfloat16):
    entries = jax.random.normal(own_key, shape, jnp.float32) * width
    return jnp.minimum(jnp.maximum(entries, -bound), bound).astype(dtype)


def setup_inputs(seed: int = 0) -> dict:
    key_list = jax.random.split(jax.random.key(seed), 4)
    return {
        "modes": draw_modes(jax.random.fold_in(key_list[3], 71), 0),
        "batch": draw_batch(jax.random.fold_in(key_list[3], 71), 0),
        "core": gaussian(key_list[2], (KB, K), KB ** -0.5, 0.21875, jnp.float32),
    }


def reference(modes, batch, core):
    hi = lax.Precision.HIGHEST
    coeffs = jnp.dot(modes.T.astype(jnp.float32), batch.astype(jnp.float32), precision=hi, preferred_element_type=jnp.float32) / ROWS
    resid = batch - jnp.dot(modes.astype(jnp.float32), coeffs.astype(jnp.float32), precision=hi, preferred_element_type=jnp.float32)
    gram = jnp.dot(resid.T.astype(jnp.float32), resid.astype(jnp.float32), precision=hi, preferred_element_type=jnp.float32) / ROWS
    lower = jnp.linalg.cholesky(gram)
    basis = jax.scipy.linalg.solve_triangular(lower, resid.T, lower=True).T
    top = jnp.dot(modes.astype(jnp.float32), core[:K].astype(jnp.float32), precision=hi, preferred_element_type=jnp.float32)
    return top + jnp.dot(basis.astype(jnp.float32), core[K:].astype(jnp.float32), precision=hi, preferred_element_type=jnp.float32)
```

```python
import functools

import jax
import jax.numpy as jnp
from jax import lax
from jax.experimental import pallas as pl
from jax.experimental.pallas import tpu as pltpu
from jax.sharding import PartitionSpec as P

MESH = pl.DeviceIdType.MESH
NZ, NY, NX = 8, 4, 4
PAIRS = ((0, 0), (0, 1), (1, 1), (0, 2), (1, 2), (2, 2))
PANELS = 2 * len(PAIRS)


def split(value):
    high = value.astype(jnp.bfloat16)
    low = (value - high.astype(jnp.float32)).astype(jnp.bfloat16)
    return high, low


def gram_kernel(modes_ref, batch_ref, gram_ref):
    @pl.when(pl.program_id(0) == 0)
    def _():
        gram_ref[...] = jnp.zeros_like(gram_ref)

    groups = (modes_ref[:, :256], modes_ref[:, 256:], batch_ref[...])
    parts = [split(group) for group in groups]
    flipped = [(high.T, low.T) for high, low in parts]
    for index, (i, j) in enumerate(PAIRS):
        high_t, low_t = flipped[i]
        high, low = parts[j]
        block = jnp.dot(high_t, low, preferred_element_type=jnp.float32)
        block += jnp.dot(low_t, high, preferred_element_type=jnp.float32)
        block += jnp.dot(high_t, high, preferred_element_type=jnp.float32)
        gram_ref[2 * index] += block[:, :128]
        gram_ref[2 * index + 1] += block[:, 128:]


def local_gram(modes, batch, tile=512):
    rows, width = modes.shape
    return pl.pallas_call(
        gram_kernel,
        grid=(rows // tile,),
        in_specs=[
            pl.BlockSpec((tile, width), lambda i: (i, 0)),
            pl.BlockSpec((tile, batch.shape[1]), lambda i: (i, 0)),
        ],
        out_specs=pl.BlockSpec((PANELS, 256, 128), lambda i: (0, 0, 0)),
        out_shape=jax.ShapeDtypeStruct((PANELS, 256, 128), jnp.float32),
        compiler_params=pltpu.CompilerParams(dimension_semantics=("arbitrary",)),
        name="gram",
    )(modes, batch)


def sum_kernel(
    part, out, from_core, half, from_first, quarter, from_second, mine, from_z,
    core_send, core_recv, first_send, first_recv, second_send, second_recv, z_send, z_recv,
    gather_second, gather_first, gather_core, arrived,
):
    gx, gy = lax.axis_index("gx"), lax.axis_index("gy")
    z, core = gx // 2, gx % 2
    y, x = gy // NX, gy % NX
    partner = (z * 2 + (1 - core), gy)
    first, second = (x, y), (y, x)

    def along(axis, index):
        return (gx, y * NX + index) if axis == 0 else (gx, index * NX + x)

    def at_z(index):
        return (index * 2 + core, gy)

    def copy(src, dst, send, recv, device):
        return pltpu.make_async_remote_copy(
            src_ref=src, dst_ref=dst, send_sem=send, recv_sem=recv,
            device_id=device, device_id_type=MESH,
        )

    barrier = pltpu.get_barrier_semaphore()
    peers = [partner]
    peers += [along(0, (x + d) % NX) for d in range(1, NX)]
    peers += [along(1, (y + d) % NY) for d in range(1, NY)]
    peers += [at_z((z + d) % NZ) for d in range(1, NZ)]
    for peer in peers:
        pl.semaphore_signal(barrier, inc=1, device_id=peer, device_id_type=MESH)
    pl.semaphore_wait(barrier, len(peers))

    sent = []

    def start(c):
        c.start()
        sent.append(c)
        return c

    core_copies = {}
    for d in (2, 1, 3, 0):
        for p in (0, 1):
            a = (first[p] + d) % 4
            core_copies[p, d] = start(copy(
                part.at[1 - core, p, a], from_core.at[p, a], core_send.at[p, d], core_recv.at[p, d], partner))

    first_copies = {}
    for d in (2, 1, 3, 0):
        for p in (0, 1):
            a = (first[p] + d) % 4
            core_copies[p, d].wait_recv()
            half[p, d] = part[core, p, a] + from_core[p, a]
            if d:
                first_copies[p, d] = start(copy(
                    half.at[p, d], from_first.at[p, d - 1], first_send.at[p, d - 1], first_recv.at[p, d - 1],
                    along(p, a)))

    second_copies = {}
    for p in (0, 1):
        for d in (2, 1, 3):
            first_copies[p, d].wait_recv()
        for d in (2, 1, 3, 0):
            b = (second[p] + d) % 4
            quarter[p, d] = (
                half[p, 0, b] + from_first[p, 0, b]) + (from_first[p, 1, b] + from_first[p, 2, b])
            if d:
                second_copies[p, d] = start(copy(
                    quarter.at[p, d], from_second.at[p, d - 1], second_send.at[p, d - 1],
                    second_recv.at[p, d - 1], along(1 - p, b)))

    for p in (0, 1):
        for d in (2, 1, 3):
            second_copies[p, d].wait_recv()
        mine[p] = (quarter[p, 0] + from_second[p, 0]) + (from_second[p, 1] + from_second[p, 2])

    z_copies = {}
    for d in (4, 3, 5, 2, 6, 1, 7):
        z_copies[d] = start(copy(
            mine, from_z.at[z], z_send.at[d - 1], z_recv.at[d - 1], at_z((z + d) % NZ)))
    from_z[z] = mine[...]
    for d in (1, 7, 2, 6, 3, 5, 4):
        z_copies[d].wait_recv()

    def place(owner, p, a, b):
        return (owner, p, a, b)

    for p in (0, 1):
        here = (core, p, first[p], second[p])
        total = from_z[0, p]
        for index in range(1, NZ):
            total = total + from_z[index, p]
        out[here] = total
        for d in (2, 1, 3):
            start(copy(out.at[here], out.at[here], gather_second.at[p, d - 1], arrived.at[here],
                       along(1 - p, (second[p] + d) % 4)))
        for d in (2, 1, 3):
            start(copy(out.at[here], out.at[here], gather_first.at[p, 0, d - 1], arrived.at[here],
                       along(p, (first[p] + d) % 4)))
        start(copy(out.at[here], out.at[here], gather_core.at[p, 0, 0], arrived.at[here], partner))

    def received(piece):
        copy(out.at[piece], out.at[piece], gather_core.at[0, 0, 0], arrived.at[piece], partner).wait_recv()

    for e in (1, 3, 2):
        for p in (0, 1):
            piece = (core, p, first[p], (second[p] + e) % 4)
            received(piece)
            for d in (2, 1, 3):
                start(copy(out.at[piece], out.at[piece], gather_first.at[p, e, d - 1], arrived.at[piece],
                           along(p, (first[p] + d) % 4)))
            start(copy(out.at[piece], out.at[piece], gather_core.at[p, 0, e], arrived.at[piece], partner))

    for e in (0, 1, 3, 2):
        for d in (1, 3, 2):
            for p in (0, 1):
                piece = (core, p, (first[p] + d) % 4, (second[p] + e) % 4)
                received(piece)
                start(copy(out.at[piece], out.at[piece], gather_core.at[p, d, e], arrived.at[piece], partner))

    for d in range(4):
        for e in range(4):
            for p in (0, 1):
                received((1 - core, p, (first[p] + d) % 4, (second[p] + e) % 4))
    for c in sent:
        c.wait_send()


def global_sum(part):
    rows = part.shape[0] * part.shape[1] // 64
    f32 = jnp.float32
    vmem = pl.BlockSpec(memory_space=pltpu.VMEM)
    dma = pltpu.SemaphoreType.DMA
    out = pl.pallas_call(
        sum_kernel,
        in_specs=[vmem],
        out_specs=vmem,
        out_shape=jax.ShapeDtypeStruct((2, 2, 4, 4, rows, 128), f32),
        scratch_shapes=[
            pltpu.VMEM((2, 4, 4, rows, 128), f32),
            pltpu.VMEM((2, 4, 4, rows, 128), f32),
            pltpu.VMEM((2, 3, 4, rows, 128), f32),
            pltpu.VMEM((2, 4, rows, 128), f32),
            pltpu.VMEM((2, 3, rows, 128), f32),
            pltpu.VMEM((2, rows, 128), f32),
            pltpu.VMEM((NZ, 2, rows, 128), f32),
            dma((2, 4)), dma((2, 4)), dma((2, 3)), dma((2, 3)), dma((2, 3)), dma((2, 3)),
            dma((NZ - 1,)), dma((NZ - 1,)),
            dma((2, 3)), dma((2, 4, 3)), dma((2, 4, 4)), dma((2, 2, 4, 4)),
        ],
        compiler_params=pltpu.CompilerParams(collective_id=0, has_side_effects=True),
        name="global_sum",
    )(part.reshape(2, 2, 4, 4, rows, 128))
    return out.reshape(part.shape)


def matmul(left, right, precision=lax.Precision.HIGHEST):
    return jnp.dot(left, right, precision=precision, preferred_element_type=jnp.float32)


def shards(modes, batch, core):
    total_rows = modes.shape[0] * lax.axis_size("gx") * lax.axis_size("gy")
    width = modes.shape[1]
    sums = global_sum(local_gram(modes, batch))
    block = {pair: jnp.concatenate([sums[2 * i], sums[2 * i + 1]], axis=1) for i, pair in enumerate(PAIRS)}
    modes_modes = jnp.block([[block[0, 0], block[0, 1]], [block[0, 1].T, block[1, 1]]])
    modes_batch = jnp.concatenate([block[0, 2], block[1, 2]], axis=0)
    coeffs = modes_batch / total_rows
    gram = (block[2, 2] - matmul(coeffs.T, 2.0 * modes_batch - matmul(modes_modes, coeffs))) / total_rows
    lower = jnp.linalg.cholesky(gram)
    inverse = jax.scipy.linalg.solve_triangular(lower, jnp.eye(lower.shape[0], dtype=jnp.float32), lower=True)
    weights = matmul(inverse.T, core[width:])
    top = core[:width] - matmul(coeffs, weights)
    high = lax.Precision.HIGH
    return matmul(modes, top, high) + matmul(batch, weights, high)


def solution(mesh):
    placed = (P(("gx", "gy"), None), P(("gx", "gy"), None), P())
    return jax.shard_map(
        shards, mesh=mesh, in_specs=placed, out_specs=P(("gx", "gy"), None), check_vma=False
    )
```

```python
import functools

import jax
import jax.numpy as jnp
from jax import lax
from jax.experimental import pallas as pl
from jax.experimental.pallas import tpu as pltpu
from jax.sharding import PartitionSpec as P

MESH = pl.DeviceIdType.MESH
NZ, NY, NX = 8, 4, 4
PAIRS = ((0, 0), (0, 1), (1, 1), (0, 2), (1, 2), (2, 2))
PANELS = 2 * len(PAIRS)
BLOCK = 64


def split(value):
    high = value.astype(jnp.bfloat16)
    low = (value - high.astype(jnp.float32)).astype(jnp.bfloat16)
    return high, low


def gram_kernel(modes_ref, batch_ref, gram_ref):
    @pl.when(pl.program_id(0) == 0)
    def _():
        gram_ref[...] = jnp.zeros_like(gram_ref)

    groups = (modes_ref[:, :256], modes_ref[:, 256:], batch_ref[...])
    parts = [split(group) for group in groups]
    flipped = [(high.T, low.T) for high, low in parts]
    for index, (i, j) in enumerate(PAIRS):
        high_t, low_t = flipped[i]
        high, low = parts[j]
        block = jnp.dot(high_t, low, preferred_element_type=jnp.float32)
        block += jnp.dot(low_t, high, preferred_element_type=jnp.float32)
        block += jnp.dot(high_t, high, preferred_element_type=jnp.float32)
        gram_ref[2 * index] += block[:, :128]
        gram_ref[2 * index + 1] += block[:, 128:]


def local_gram(modes, batch, tile=512):
    rows, width = modes.shape
    return pl.pallas_call(
        gram_kernel,
        grid=(rows // tile,),
        in_specs=[
            pl.BlockSpec((tile, width), lambda i: (i, 0)),
            pl.BlockSpec((tile, batch.shape[1]), lambda i: (i, 0)),
        ],
        out_specs=pl.BlockSpec((PANELS, 256, 128), lambda i: (0, 0, 0)),
        out_shape=jax.ShapeDtypeStruct((PANELS, 256, 128), jnp.float32),
        compiler_params=pltpu.CompilerParams(dimension_semantics=("arbitrary",)),
        name="gram",
    )(modes, batch)


def sum_kernel(
    part, out, from_core, half, from_first, quarter, from_second, mine, from_z,
    core_send, core_recv, first_send, first_recv, second_send, second_recv, z_send, z_recv,
    gather_second, gather_first, gather_core, arrived,
):
    gx, gy = lax.axis_index("gx"), lax.axis_index("gy")
    z, core = gx // 2, gx % 2
    y, x = gy // NX, gy % NX
    partner = (z * 2 + (1 - core), gy)
    first, second = (x, y), (y, x)

    def along(axis, index):
        return (gx, y * NX + index) if axis == 0 else (gx, index * NX + x)

    def at_z(index):
        return (index * 2 + core, gy)

    def copy(src, dst, send, recv, device):
        return pltpu.make_async_remote_copy(
            src_ref=src, dst_ref=dst, send_sem=send, recv_sem=recv,
            device_id=device, device_id_type=MESH,
        )

    barrier = pltpu.get_barrier_semaphore()
    peers = [partner]
    peers += [along(0, (x + d) % NX) for d in range(1, NX)]
    peers += [along(1, (y + d) % NY) for d in range(1, NY)]
    peers += [at_z((z + d) % NZ) for d in range(1, NZ)]
    for peer in peers:
        pl.semaphore_signal(barrier, inc=1, device_id=peer, device_id_type=MESH)
    pl.semaphore_wait(barrier, len(peers))

    sent = []

    def start(c):
        c.start()
        sent.append(c)
        return c

    core_copies = {}
    for d in (2, 1, 3, 0):
        for p in (0, 1):
            a = (first[p] + d) % 4
            core_copies[p, d] = start(copy(
                part.at[1 - core, p, a], from_core.at[p, a], core_send.at[p, d], core_recv.at[p, d], partner))

    first_copies = {}
    for d in (2, 1, 3, 0):
        for p in (0, 1):
            a = (first[p] + d) % 4
            core_copies[p, d].wait_recv()
            half[p, d] = part[core, p, a] + from_core[p, a]
            if d:
                first_copies[p, d] = start(copy(
                    half.at[p, d], from_first.at[p, d - 1], first_send.at[p, d - 1], first_recv.at[p, d - 1],
                    along(p, a)))

    second_copies = {}
    for p in (0, 1):
        for d in (2, 1, 3):
            first_copies[p, d].wait_recv()
        for d in (2, 1, 3, 0):
            b = (second[p] + d) % 4
            quarter[p, d] = (
                half[p, 0, b] + from_first[p, 0, b]) + (from_first[p, 1, b] + from_first[p, 2, b])
            if d:
                second_copies[p, d] = start(copy(
                    quarter.at[p, d], from_second.at[p, d - 1], second_send.at[p, d - 1],
                    second_recv.at[p, d - 1], along(1 - p, b)))

    for p in (0, 1):
        for d in (2, 1, 3):
            second_copies[p, d].wait_recv()
        mine[p] = (quarter[p, 0] + from_second[p, 0]) + (from_second[p, 1] + from_second[p, 2])

    z_copies = {}
    for d in (4, 3, 5, 2, 6, 1, 7):
        z_copies[d] = start(copy(
            mine, from_z.at[z], z_send.at[d - 1], z_recv.at[d - 1], at_z((z + d) % NZ)))
    from_z[z] = mine[...]
    for d in (1, 7, 2, 6, 3, 5, 4):
        z_copies[d].wait_recv()

    def place(owner, p, a, b):
        return (owner, p, a, b)

    for p in (0, 1):
        here = (core, p, first[p], second[p])
        total = from_z[0, p]
        for index in range(1, NZ):
            total = total + from_z[index, p]
        out[here] = total
        for d in (2, 1, 3):
            start(copy(out.at[here], out.at[here], gather_second.at[p, d - 1], arrived.at[here],
                       along(1 - p, (second[p] + d) % 4)))
        for d in (2, 1, 3):
            start(copy(out.at[here], out.at[here], gather_first.at[p, 0, d - 1], arrived.at[here],
                       along(p, (first[p] + d) % 4)))
        start(copy(out.at[here], out.at[here], gather_core.at[p, 0, 0], arrived.at[here], partner))

    def received(piece):
        copy(out.at[piece], out.at[piece], gather_core.at[0, 0, 0], arrived.at[piece], partner).wait_recv()

    for e in (1, 3, 2):
        for p in (0, 1):
            piece = (core, p, first[p], (second[p] + e) % 4)
            received(piece)
            for d in (2, 1, 3):
                start(copy(out.at[piece], out.at[piece], gather_first.at[p, e, d - 1], arrived.at[piece],
                           along(p, (first[p] + d) % 4)))
            start(copy(out.at[piece], out.at[piece], gather_core.at[p, 0, e], arrived.at[piece], partner))

    for e in (0, 1, 3, 2):
        for d in (1, 3, 2):
            for p in (0, 1):
                piece = (core, p, (first[p] + d) % 4, (second[p] + e) % 4)
                received(piece)
                start(copy(out.at[piece], out.at[piece], gather_core.at[p, d, e], arrived.at[piece], partner))

    for d in range(4):
        for e in range(4):
            for p in (0, 1):
                received((1 - core, p, (first[p] + d) % 4, (second[p] + e) % 4))
    for c in sent:
        c.wait_send()


def global_sum(part):
    rows = part.shape[0] * part.shape[1] // 64
    f32 = jnp.float32
    vmem = pl.BlockSpec(memory_space=pltpu.VMEM)
    dma = pltpu.SemaphoreType.DMA
    out = pl.pallas_call(
        sum_kernel,
        in_specs=[vmem],
        out_specs=vmem,
        out_shape=jax.ShapeDtypeStruct((2, 2, 4, 4, rows, 128), f32),
        scratch_shapes=[
            pltpu.VMEM((2, 4, 4, rows, 128), f32),
            pltpu.VMEM((2, 4, 4, rows, 128), f32),
            pltpu.VMEM((2, 3, 4, rows, 128), f32),
            pltpu.VMEM((2, 4, rows, 128), f32),
            pltpu.VMEM((2, 3, rows, 128), f32),
            pltpu.VMEM((2, rows, 128), f32),
            pltpu.VMEM((NZ, 2, rows, 128), f32),
            dma((2, 4)), dma((2, 4)), dma((2, 3)), dma((2, 3)), dma((2, 3)), dma((2, 3)),
            dma((NZ - 1,)), dma((NZ - 1,)),
            dma((2, 3)), dma((2, 4, 3)), dma((2, 4, 4)), dma((2, 2, 4, 4)),
        ],
        compiler_params=pltpu.CompilerParams(collective_id=0, has_side_effects=True),
        name="global_sum",
    )(part.reshape(2, 2, 4, 4, rows, 128))
    return out.reshape(part.shape)


def exact_dot(a, b, dims=((1,), (0,))):
    return lax.dot_general(a, b, (dims, ((), ())), precision=lax.Precision.HIGHEST, preferred_element_type=jnp.float32)

def lanes(value, index):
    return jnp.broadcast_to(value[:, index:index + 1], value.shape)

def row_of(value, index):
    return jnp.broadcast_to(value[index:index + 1, :], value.shape)

def eliminate(tiles, offset):
    shape = tiles[0].shape
    sub = lax.broadcasted_iota(jnp.int32, shape, 0)
    scales = []
    for g in range(len(tiles)):
        w = tiles[g]
        c = [lanes(w, offset + 8 * g + j) for j in range(8)]
        rows, inv, s = [], [], {}
        pivots = jnp.ones(shape, jnp.float32)
        for j in range(8):
            row = row_of(w, j)
            pivot = row_of(c[j], j)
            r = 1.0 / pivot
            pivots = jnp.where(sub == j, pivot, pivots)
            m = jnp.where(sub > j, c[j] * r, 0.0)
            w = w - m * row
            for k in range(j + 1, 8):
                s[j, k] = row_of(c[k], j)
                c[k] = c[k] - m * s[j, k]
            rows.append(row)
            inv.append(r)
        tiles[g] = w
        scales.append(lax.rsqrt(pivots))
        for h in range(g + 1, len(tiles)):
            v = tiles[h]
            c = [lanes(v, offset + 8 * g + j) for j in range(8)]
            for j in range(8):
                m = c[j] * inv[j]
                v = v - m * rows[j]
                for k in range(j + 1, 8):
                    c[k] = c[k] - m * s[j, k]
            tiles[h] = v
    return [t * q for t, q in zip(tiles, scales)]


def factor(aug):
    n = aug.shape[0]
    for d in range(n // BLOCK):
        o = BLOCK * d
        tile = o // 128 * 128
        odd = d % 2
        block = aug[o:o + BLOCK, tile:tile + 128]
        lane = lax.broadcasted_iota(jnp.int32, (BLOCK, 128), 1)
        row = lax.broadcasted_iota(jnp.int32, (BLOCK, 128), 0)
        eye = jnp.where(lane == row + (0 if odd else 64), 1.0, 0.0)
        w = jnp.where((lane >= 64) if odd else (lane < 64), block, eye)
        tiles = eliminate([w[8 * g:8 * g + 8] for g in range(BLOCK // 8)], 64 if odd else 0)
        w = jnp.concatenate(tiles, axis=0)
        if not odd:
            w = pltpu.roll(w, 64, 1)
        z = w[:, :64]
        new = exact_dot(z, aug[o:o + BLOCK, :])
        aug[o:o + BLOCK, :] = new
        if o + BLOCK < n:
            rest = new[:, :n]
            upd = exact_dot(rest, new, ((0,), (0,)))
            aug[o + BLOCK:, :] = aug[o + BLOCK:, :] - upd[o + BLOCK:, :]

def update_kernel(total_rows, sums_ref, core_ref, modes_ref, batch_ref, out_ref, aug, high, low):
    width = modes_ref.shape[1]
    n = batch_ref.shape[1]

    @pl.when(pl.program_id(0) == 0)
    def _():
        def block(index):
            return jnp.concatenate([sums_ref[2 * index], sums_ref[2 * index + 1]], axis=1)

        first, second = block(3), block(4)
        coeffs = (first * (1.0 / total_rows), second * (1.0 / total_rows))
        mixed = block(1)
        product_first = exact_dot(block(0), coeffs[0]) + exact_dot(mixed, coeffs[1])
        product_second = exact_dot(mixed, coeffs[0], ((0,), (0,))) + exact_dot(block(2), coeffs[1])
        gram = block(5) - exact_dot(coeffs[0], 2.0 * first - product_first, ((0,), (0,)))
        gram = gram - exact_dot(coeffs[1], 2.0 * second - product_second, ((0,), (0,)))
        aug[:, :n] = gram * (1.0 / total_rows)
        row = lax.broadcasted_iota(jnp.int32, (n, n), 0)
        column = lax.broadcasted_iota(jnp.int32, (n, n), 1)
        aug[:, n:] = jnp.where(row == column, 1.0, 0.0)
        factor(aug)
        weights = exact_dot(aug[:, n:], core_ref[width:, :], ((0,), (0,)))
        high[width:, :], low[width:, :] = split(weights)
        for i in range(width // n):
            top = core_ref[n * i:n * (i + 1), :] - exact_dot(coeffs[i], weights)
            high[n * i:n * (i + 1), :], low[n * i:n * (i + 1), :] = split(top)

    modes_high, modes_low = split(modes_ref[...])
    batch_high, batch_low = split(batch_ref[...])

    def times(left, right):
        return jnp.dot(left, right, preferred_element_type=jnp.float32)

    small = times(modes_low, high[:width, :]) + times(batch_low, high[width:, :])
    small += times(modes_high, low[:width, :]) + times(batch_high, low[width:, :])
    out_ref[...] = small + times(modes_high, high[:width, :]) + times(batch_high, high[width:, :])


def update(sums, core, modes, batch, total_rows, tile=256):
    rows, width = modes.shape
    n = batch.shape[1]
    return pl.pallas_call(
        functools.partial(update_kernel, total_rows),
        grid=(rows // tile,),
        in_specs=[
            pl.BlockSpec(sums.shape, lambda i: (0, 0, 0), pipeline_mode=pl.Buffered(1)),
            pl.BlockSpec(core.shape, lambda i: (0, 0), pipeline_mode=pl.Buffered(1)),
            pl.BlockSpec((tile, width), lambda i: (i, 0)),
            pl.BlockSpec((tile, n), lambda i: (i, 0)),
        ],
        out_specs=pl.BlockSpec((tile, width), lambda i: (i, 0)),
        out_shape=jax.ShapeDtypeStruct((rows, width), jnp.float32),
        scratch_shapes=[
            pltpu.VMEM((n, 2 * n), jnp.float32),
            pltpu.VMEM(core.shape, jnp.bfloat16),
            pltpu.VMEM(core.shape, jnp.bfloat16),
        ],
        compiler_params=pltpu.CompilerParams(dimension_semantics=("arbitrary",)),
        name="update",
    )(sums, core, modes, batch)


def shards(modes, batch, core):
    total_rows = modes.shape[0] * lax.axis_size("gx") * lax.axis_size("gy")
    return update(global_sum(local_gram(modes, batch)), core, modes, batch, total_rows)


def solution(mesh):
    placed = (P(("gx", "gy"), None), P(("gx", "gy"), None), P())
    return jax.shard_map(
        shards, mesh=mesh, in_specs=placed, out_specs=P(("gx", "gy"), None), check_vma=False
    )
```

```python
import functools

import jax
import jax.numpy as jnp
from jax import lax
from jax.experimental import pallas as pl
from jax.experimental.pallas import tpu as pltpu
from jax.sharding import PartitionSpec as P

MESH = pl.DeviceIdType.MESH
NZ, NY, NX = 8, 4, 4
PAIRS = ((0, 0), (0, 1), (1, 1), (0, 2), (1, 2), (2, 2))
BLOCK = 64
GROUPS = ((0, 3), (3, 6))


def split(value):
    high = value.astype(jnp.bfloat16)
    low = (value - high.astype(jnp.float32)).astype(jnp.bfloat16)
    return high, low


CHUNKS = 4


def load_split(modes, batch, raw_modes, raw_batch, load_sem, parts, flipped):
    rows = raw_modes.shape[0] // CHUNKS
    loads = []
    for i in range(CHUNKS):
        here = pl.ds(i * rows, rows)
        loads.append((
            pltpu.make_async_copy(modes.at[here], raw_modes.at[here], load_sem.at[0, i]),
            pltpu.make_async_copy(batch.at[here], raw_batch.at[here], load_sem.at[1, i])))
        for load in loads[-1]:
            load.start()
    for i in range(CHUNKS):
        here = pl.ds(i * rows, rows)
        for load in loads[i]:
            load.wait()
        for g in range(3):
            group = raw_modes[here, 256 * g:256 * (g + 1)] if g < 2 else raw_batch[here, :]
            high, low = split(group)
            parts[0, g, here] = high
            parts[1, g, here] = low
            flipped[g, :256, here] = high.T
            flipped[g, 256:, here] = low.T


def gram_block(i, j, parts, flipped):
    both = jnp.dot(flipped[i], parts[0, j], preferred_element_type=jnp.float32)
    mixed = both[256:]
    if i == j:
        return both[:256] + (mixed + mixed.T)
    other = jnp.dot(flipped[i, :256], parts[1, j], preferred_element_type=jnp.float32)
    return both[:256] + (mixed + other)


def sum_kernel(
    modes, batch, out, raw_modes, raw_batch, parts, flipped,
    part, from_core, half, from_first, quarter, from_second, mine, from_near, three, pair, from_far, load_sem,
    core_send, core_recv, first_send, first_recv, second_send, second_recv, near_send, near_recv, far_send, far_recv,
    gather_second, gather_first, gather_core, arrived,
):
    gx, gy = lax.axis_index("gx"), lax.axis_index("gy")
    z, core = gx // 2, gx % 2
    y, x = gy // NX, gy % NX
    partner = (z * 2 + (1 - core), gy)
    first, second = (x, y), (y, x)

    def along(axis, index):
        return (gx, y * NX + index) if axis == 0 else (gx, index * NX + x)

    def at_z(index):
        return (index * 2 + core, gy)

    def copy(src, dst, send, recv, device):
        return pltpu.make_async_remote_copy(
            src_ref=src, dst_ref=dst, send_sem=send, recv_sem=recv,
            device_id=device, device_id_type=MESH,
        )

    barrier = pltpu.get_barrier_semaphore()
    peers = [partner]
    peers += [along(0, (x + d) % NX) for d in range(1, NX)]
    peers += [along(1, (y + d) % NY) for d in range(1, NY)]
    peers += [at_z((z + d) % NZ) for d in (1, 2, 3, 5, 6, 7)]
    for peer in peers:
        pl.semaphore_signal(barrier, inc=1, device_id=peer, device_id_type=MESH)

    sent = []

    def start(c):
        c.start()
        sent.append(c)
        return c

    first_copies = {}

    def keep_half(t, core_copy):
        core_copy.wait_recv()
        kept = part[t, core] + from_core[t]
        for p in (0, 1):
            for a in range(4):
                half[p, a, t] = kept[p, a]

    def along_first(group):
        begin, end = GROUPS[group]
        for d in (2, 1, 3):
            for p in (0, 1):
                a = (first[p] + d) % 4
                first_copies[group, p, d] = start(copy(
                    half.at[p, a, pl.ds(begin, end - begin)], from_first.at[p, d - 1, pl.ds(begin, end - begin)],
                    first_send.at[group, p, d - 1], first_recv.at[group, p, d - 1], along(p, a)))

    load_split(modes, batch, raw_modes, raw_batch, load_sem, parts, flipped)
    pending = None
    for t, (i, j) in enumerate(PAIRS):
        block = gram_block(i, j, parts, flipped)
        for h in range(2):
            part[t, h] = block[:, 128 * h:128 * (h + 1)].reshape(2, 4, 4, 8, 128)
        if t == 0:
            pl.semaphore_wait(barrier, len(peers))
        core_copy = start(copy(
            part.at[t, 1 - core], from_core.at[t], core_send.at[t], core_recv.at[t], partner))
        if pending is not None:
            keep_half(t - 1, pending)
            for group, (begin, end) in enumerate(GROUPS):
                if end == t:
                    along_first(group)
        pending = core_copy
    keep_half(len(PAIRS) - 1, pending)
    along_first(len(GROUPS) - 1)

    second_copies = {}
    for p in (0, 1):
        for group in range(len(GROUPS)):
            for d in (2, 1, 3):
                first_copies[group, p, d].wait_recv()
        for d in (2, 1, 3, 0):
            b = (second[p] + d) % 4
            for t in range(len(PAIRS)):
                quarter[p, d, 8 * t:8 * (t + 1)] = (half[p, first[p], t, b] + from_first[p, 0, t, b]) + (
                    from_first[p, 1, t, b] + from_first[p, 2, t, b])
            if d:
                second_copies[p, d] = start(copy(
                    quarter.at[p, d], from_second.at[p, d - 1], second_send.at[p, d - 1],
                    second_recv.at[p, d - 1], along(1 - p, b)))

    for p in (0, 1):
        for d in (2, 1, 3):
            second_copies[p, d].wait_recv()
        mine[p] = (quarter[p, 0] + from_second[p, 0]) + (from_second[p, 1] + from_second[p, 2])

    z_copies = {}
    for side in (0, 1):
        z_copies[side] = start(copy(
            mine, from_near.at[side], near_send.at[side], near_recv.at[side], at_z((z + (1, 7)[side]) % NZ)))
    for side in (0, 1):
        z_copies[side].wait_recv()
    far_copies = []
    for p in (0, 1):
        two = mine[p] + from_near[1 - p, p]
        pair[p] = two
        three[p] = two + from_near[p, p]
        far_copies.append(start(copy(
            three.at[p], from_far.at[p, 0], far_send.at[p, 0], far_recv.at[p, 0], at_z((z + (3, 5)[p]) % NZ))))
        far_copies.append(start(copy(
            pair.at[p], from_far.at[p, 1], far_send.at[p, 1], far_recv.at[p, 1], at_z((z + (6, 2)[p]) % NZ))))
    for c in far_copies:
        c.wait_recv()

    for p in (0, 1):
        here = (core, p, first[p], second[p])
        out[here] = three[p] + (from_far[p, 0] + from_far[p, 1])
        for d in (2, 1, 3):
            start(copy(out.at[here], out.at[here], gather_second.at[p, d - 1], arrived.at[here],
                       along(1 - p, (second[p] + d) % 4)))
        for d in (2, 1, 3):
            start(copy(out.at[here], out.at[here], gather_first.at[p, 0, d - 1], arrived.at[here],
                       along(p, (first[p] + d) % 4)))
        start(copy(out.at[here], out.at[here], gather_core.at[p, 0, 0], arrived.at[here], partner))

    def received(piece):
        copy(out.at[piece], out.at[piece], gather_core.at[0, 0, 0], arrived.at[piece], partner).wait_recv()

    for e in (1, 3, 2):
        for p in (0, 1):
            piece = (core, p, first[p], (second[p] + e) % 4)
            received(piece)
            for d in (2, 1, 3):
                start(copy(out.at[piece], out.at[piece], gather_first.at[p, e, d - 1], arrived.at[piece],
                           along(p, (first[p] + d) % 4)))
            start(copy(out.at[piece], out.at[piece], gather_core.at[p, 0, e], arrived.at[piece], partner))

    for e in (0, 1, 3, 2):
        for d in (1, 3, 2):
            for p in (0, 1):
                piece = (core, p, (first[p] + d) % 4, (second[p] + e) % 4)
                received(piece)
                start(copy(out.at[piece], out.at[piece], gather_core.at[p, d, e], arrived.at[piece], partner))

    for d in range(4):
        for e in range(4):
            for p in (0, 1):
                received((1 - core, p, (first[p] + d) % 4, (second[p] + e) % 4))
    for c in sent:
        c.wait_send()


def gram_sum(modes, batch):
    rows = 8 * len(PAIRS)
    blocks = len(PAIRS)
    f32, b16 = jnp.float32, jnp.bfloat16
    dma = pltpu.SemaphoreType.DMA
    return pl.pallas_call(
        sum_kernel,
        in_specs=[pl.BlockSpec(memory_space=pl.ANY)] * 2,
        out_specs=pl.BlockSpec(memory_space=pltpu.VMEM),
        out_shape=jax.ShapeDtypeStruct((2, 2, 4, 4, rows, 128), f32),
        scratch_shapes=[
            pltpu.VMEM(modes.shape, f32),
            pltpu.VMEM(batch.shape, f32),
            pltpu.VMEM((2, 3, modes.shape[0], 256), b16),
            pltpu.VMEM((3, 512, modes.shape[0]), b16),
            pltpu.VMEM((blocks, 2, 2, 4, 4, 8, 128), f32),
            pltpu.VMEM((blocks, 2, 4, 4, 8, 128), f32),
            pltpu.VMEM((2, 4, blocks, 4, 8, 128), f32),
            pltpu.VMEM((2, 3, blocks, 4, 8, 128), f32),
            pltpu.VMEM((2, 4, rows, 128), f32),
            pltpu.VMEM((2, 3, rows, 128), f32),
            pltpu.VMEM((2, rows, 128), f32),
            pltpu.VMEM((2, 2, rows, 128), f32),
            pltpu.VMEM((2, rows, 128), f32),
            pltpu.VMEM((2, rows, 128), f32),
            pltpu.VMEM((2, 2, rows, 128), f32),
            dma((2, CHUNKS)),
            dma((blocks,)), dma((blocks,)), dma((len(GROUPS), 2, 3)), dma((len(GROUPS), 2, 3)), dma((2, 3)), dma((2, 3)),
            dma((2,)), dma((2,)), dma((2, 2)), dma((2, 2)),
            dma((2, 3)), dma((2, 4, 3)), dma((2, 4, 4)), dma((2, 2, 4, 4)),
        ],
        compiler_params=pltpu.CompilerParams(collective_id=0, has_side_effects=True),
        name="gram_sum",
    )(modes, batch)


def exact_dot(a, b, dims=((1,), (0,))):
    (a_high, a_low), (b_high, b_low) = split(a), split(b)

    def dot(left, right):
        return lax.dot_general(left, right, (dims, ((), ())), preferred_element_type=jnp.float32)

    return dot(a_high, b_high) + (dot(a_low, b_high) + dot(a_high, b_low))


def lanes(value, index):
    return jnp.broadcast_to(value[:, index:index + 1], value.shape)

def row_of(value, index):
    return jnp.broadcast_to(value[index:index + 1, :], value.shape)

def eliminate(tiles, offset):
    shape = tiles[0].shape
    sub = lax.broadcasted_iota(jnp.int32, shape, 0)
    scales = []
    for g in range(len(tiles)):
        w = tiles[g]
        c = [lanes(w, offset + 8 * g + j) for j in range(8)]
        rows, inv, s = [], [], {}
        pivots = jnp.ones(shape, jnp.float32)
        for j in range(8):
            row = row_of(w, j)
            pivot = row_of(c[j], j)
            r = 1.0 / pivot
            pivots = jnp.where(sub == j, pivot, pivots)
            m = jnp.where(sub > j, c[j] * r, 0.0)
            w = w - m * row
            for k in range(j + 1, 8):
                s[j, k] = row_of(c[k], j)
                c[k] = c[k] - m * s[j, k]
            rows.append(row)
            inv.append(r)
        tiles[g] = w
        scales.append(lax.rsqrt(pivots))
        for h in range(g + 1, len(tiles)):
            v = tiles[h]
            c = [lanes(v, offset + 8 * g + j) for j in range(8)]
            for j in range(8):
                m = c[j] * inv[j]
                v = v - m * rows[j]
                for k in range(j + 1, 8):
                    c[k] = c[k] - m * s[j, k]
            tiles[h] = v
    return [t * q for t, q in zip(tiles, scales)]


def factor(aug):
    n = aug.shape[0]
    for d in range(n // BLOCK):
        o = BLOCK * d
        tile = o // 128 * 128
        odd = d % 2
        block = aug[o:o + BLOCK, tile:tile + 128]
        lane = lax.broadcasted_iota(jnp.int32, (BLOCK, 128), 1)
        row = lax.broadcasted_iota(jnp.int32, (BLOCK, 128), 0)
        eye = jnp.where(lane == row + (0 if odd else 64), 1.0, 0.0)
        w = jnp.where((lane >= 64) if odd else (lane < 64), block, eye)
        tiles = eliminate([w[8 * g:8 * g + 8] for g in range(BLOCK // 8)], 64 if odd else 0)
        w = jnp.concatenate(tiles, axis=0)
        if not odd:
            w = pltpu.roll(w, 64, 1)
        z = w[:, :64]
        new = exact_dot(z, aug[o:o + BLOCK, :])
        aug[o:o + BLOCK, :] = new
        if o + BLOCK < n:
            rest = new[:, :n]
            upd = exact_dot(rest, new, ((0,), (0,)))
            aug[o + BLOCK:, :] = aug[o + BLOCK:, :] - upd[o + BLOCK:, :]

def update_kernel(total_rows, sums_ref, core_ref, modes_ref, batch_ref, out_ref, aug, high, low):
    width = modes_ref.shape[1]
    n = batch_ref.shape[1]

    @pl.when(pl.program_id(0) == 0)
    def _():
        def block(index):
            panels = [sums_ref[h, :, :, :, 8 * index:8 * (index + 1), :].reshape(n, n // 2) for h in range(2)]
            return jnp.concatenate(panels, axis=1)

        first, second = block(3), block(4)
        coeffs = (first * (1.0 / total_rows), second * (1.0 / total_rows))
        mixed = block(1)
        product_first = exact_dot(block(0), coeffs[0]) + exact_dot(mixed, coeffs[1])
        product_second = exact_dot(mixed, coeffs[0], ((0,), (0,))) + exact_dot(block(2), coeffs[1])
        gram = block(5) - exact_dot(coeffs[0], 2.0 * first - product_first, ((0,), (0,)))
        gram = gram - exact_dot(coeffs[1], 2.0 * second - product_second, ((0,), (0,)))
        aug[:, :n] = gram * (1.0 / total_rows)
        row = lax.broadcasted_iota(jnp.int32, (n, n), 0)
        column = lax.broadcasted_iota(jnp.int32, (n, n), 1)
        aug[:, n:] = jnp.where(row == column, 1.0, 0.0)
        factor(aug)
        weights = exact_dot(aug[:, n:], core_ref[width:, :], ((0,), (0,)))
        high[width:, :], low[width:, :] = split(weights)
        for i in range(width // n):
            top = core_ref[n * i:n * (i + 1), :] - exact_dot(coeffs[i], weights)
            high[n * i:n * (i + 1), :], low[n * i:n * (i + 1), :] = split(top)

    values = [split(value) for value in (modes_ref[:, :n], modes_ref[:, n:], batch_ref[...])]
    stacked = jnp.concatenate(
        [jnp.concatenate([v[half] for v in values], axis=1) for half in (0, 1)], axis=0)
    rows = out_ref.shape[0]
    for i in range(width // n):
        columns = slice(n * i, n * (i + 1))
        both = jnp.dot(stacked, high[:, columns], preferred_element_type=jnp.float32)
        other = jnp.dot(stacked[:rows], low[:, columns], preferred_element_type=jnp.float32)
        out_ref[:, columns] = both[:rows] + (both[rows:] + other)


def update(sums, core, modes, batch, total_rows, tile=512):
    rows, width = modes.shape
    n = batch.shape[1]
    return pl.pallas_call(
        functools.partial(update_kernel, total_rows),
        grid=(rows // tile,),
        in_specs=[
            pl.BlockSpec(sums.shape, lambda i: (0,) * 6, pipeline_mode=pl.Buffered(1)),
            pl.BlockSpec(core.shape, lambda i: (0, 0), pipeline_mode=pl.Buffered(1)),
            pl.BlockSpec((tile, width), lambda i: (i, 0)),
            pl.BlockSpec((tile, n), lambda i: (i, 0)),
        ],
        out_specs=pl.BlockSpec((tile, width), lambda i: (i, 0)),
        out_shape=jax.ShapeDtypeStruct((rows, width), jnp.float32),
        scratch_shapes=[
            pltpu.VMEM((n, 2 * n), jnp.float32),
            pltpu.VMEM(core.shape, jnp.bfloat16),
            pltpu.VMEM(core.shape, jnp.bfloat16),
        ],
        compiler_params=pltpu.CompilerParams(dimension_semantics=("arbitrary",)),
        name="update",
    )(sums, core, modes, batch)


def shards(modes, batch, core):
    total_rows = modes.shape[0] * lax.axis_size("gx") * lax.axis_size("gy")
    return update(gram_sum(modes, batch), core, modes, batch, total_rows)


def solution(mesh):
    placed = (P(("gx", "gy"), None), P(("gx", "gy"), None), P())
    return jax.shard_map(
        shards, mesh=mesh, in_specs=placed, out_specs=P(("gx", "gy"), None), check_vma=False
    )
```

```python
import functools

import jax
import jax.numpy as jnp
from jax import lax
from jax.experimental import pallas as pl
from jax.experimental.pallas import tpu as pltpu
from jax.sharding import PartitionSpec as P

MESH = pl.DeviceIdType.MESH
NZ, NY, NX = 8, 4, 4
PAIRS = ((0, 0), (0, 1), (1, 1), (0, 2), (1, 2), (2, 2))
BLOCK = 64
GROUPS = ((0, 3), (3, 6))


def split(value):
    high = value.astype(jnp.bfloat16)
    low = (value - high.astype(jnp.float32)).astype(jnp.bfloat16)
    return high, low


def split_group(g, modes, batch, parts, flipped):
    rows = modes.shape[0]
    step = rows // 4
    for i in range(4):
        here = pl.ds(i * step, step)
        high, low = split(modes[here, 256 * g:256 * (g + 1)] if g < 2 else batch[here, :])
        parts[0, g, here] = high
        parts[1, g, here] = low
        flipped[g, :256, here] = high.T
        flipped[g, 256:, here] = low.T


def gram_block(i, j, parts, flipped):
    both = jnp.dot(flipped[i], parts[0, j], preferred_element_type=jnp.float32)
    mixed = both[256:]
    if i == j:
        return both[:256] + (mixed + mixed.T)
    other = jnp.dot(flipped[i, :256], parts[1, j], preferred_element_type=jnp.float32)
    return both[:256] + (mixed + other)


def sum_kernel(
    modes, batch, out, parts, flipped,
    part, from_core, half, from_first, quarter, from_second, mine, from_near, three, pair, from_far,
    core_send, core_recv, first_send, first_recv, second_send, second_recv, near_send, near_recv, far_send, far_recv,
    gather_second, gather_first, gather_core, arrived,
):
    gx, gy = lax.axis_index("gx"), lax.axis_index("gy")
    z, core = gx // 2, gx % 2
    y, x = gy // NX, gy % NX
    partner = (z * 2 + (1 - core), gy)
    first, second = (x, y), (y, x)

    def along(axis, index):
        return (gx, y * NX + index) if axis == 0 else (gx, index * NX + x)

    def at_z(index):
        return (index * 2 + core, gy)

    def copy(src, dst, send, recv, device):
        return pltpu.make_async_remote_copy(
            src_ref=src, dst_ref=dst, send_sem=send, recv_sem=recv,
            device_id=device, device_id_type=MESH,
        )

    barrier = pltpu.get_barrier_semaphore()
    peers = [partner]
    peers += [along(0, (x + d) % NX) for d in range(1, NX)]
    peers += [along(1, (y + d) % NY) for d in range(1, NY)]
    peers += [at_z((z + d) % NZ) for d in (1, 2, 3, 5, 6, 7)]
    for peer in peers:
        pl.semaphore_signal(barrier, inc=1, device_id=peer, device_id_type=MESH)

    sent = []

    def start(c):
        c.start()
        sent.append(c)
        return c

    first_copies = {}

    def keep_half(t, core_copy):
        core_copy.wait_recv()
        kept = part[t, core] + from_core[t]
        for p in (0, 1):
            for a in range(4):
                half[p, a, t] = kept[p, a]

    def along_first(group):
        begin, end = GROUPS[group]
        for d in (2, 1, 3):
            for p in (0, 1):
                a = (first[p] + d) % 4
                first_copies[group, p, d] = start(copy(
                    half.at[p, a, pl.ds(begin, end - begin)], from_first.at[p, d - 1, pl.ds(begin, end - begin)],
                    first_send.at[group, p, d - 1], first_recv.at[group, p, d - 1], along(p, a)))

    split_group(0, modes, batch, parts, flipped)
    pending = None
    for t, (i, j) in enumerate(PAIRS):
        if t < 2:
            split_group(t + 1, modes, batch, parts, flipped)
        block = gram_block(i, j, parts, flipped)
        for h in range(2):
            part[t, h] = block[:, 128 * h:128 * (h + 1)].reshape(2, 4, 4, 8, 128)
        if t == 0:
            pl.semaphore_wait(barrier, len(peers))
        core_copy = start(copy(
            part.at[t, 1 - core], from_core.at[t], core_send.at[t], core_recv.at[t], partner))
        if pending is not None:
            keep_half(t - 1, pending)
            for group, (begin, end) in enumerate(GROUPS):
                if end == t:
                    along_first(group)
        pending = core_copy
    keep_half(len(PAIRS) - 1, pending)
    along_first(len(GROUPS) - 1)

    second_copies = {}
    for p in (0, 1):
        for group in range(len(GROUPS)):
            for d in (2, 1, 3):
                first_copies[group, p, d].wait_recv()
        for d in (2, 1, 3, 0):
            b = (second[p] + d) % 4
            for t in range(len(PAIRS)):
                quarter[p, d, 8 * t:8 * (t + 1)] = (half[p, first[p], t, b] + from_first[p, 0, t, b]) + (
                    from_first[p, 1, t, b] + from_first[p, 2, t, b])
            if d:
                second_copies[p, d] = start(copy(
                    quarter.at[p, d], from_second.at[p, d - 1], second_send.at[p, d - 1],
                    second_recv.at[p, d - 1], along(1 - p, b)))

    for p in (0, 1):
        for d in (2, 1, 3):
            second_copies[p, d].wait_recv()
        mine[p] = (quarter[p, 0] + from_second[p, 0]) + (from_second[p, 1] + from_second[p, 2])

    z_copies = {}
    for side in (0, 1):
        z_copies[side] = start(copy(
            mine, from_near.at[side], near_send.at[side], near_recv.at[side], at_z((z + (1, 7)[side]) % NZ)))
    for side in (0, 1):
        z_copies[side].wait_recv()
    far_copies = []
    for p in (0, 1):
        two = mine[p] + from_near[1 - p, p]
        pair[p] = two
        three[p] = two + from_near[p, p]
        far_copies.append(start(copy(
            three.at[p], from_far.at[p, 0], far_send.at[p, 0], far_recv.at[p, 0], at_z((z + (3, 5)[p]) % NZ))))
        far_copies.append(start(copy(
            pair.at[p], from_far.at[p, 1], far_send.at[p, 1], far_recv.at[p, 1], at_z((z + (6, 2)[p]) % NZ))))
    for c in far_copies:
        c.wait_recv()

    for p in (0, 1):
        here = (core, p, first[p], second[p])
        out[here] = three[p] + (from_far[p, 0] + from_far[p, 1])
        for d in (2, 1, 3):
            start(copy(out.at[here], out.at[here], gather_second.at[p, d - 1], arrived.at[here],
                       along(1 - p, (second[p] + d) % 4)))
        for d in (2, 1, 3):
            start(copy(out.at[here], out.at[here], gather_first.at[p, 0, d - 1], arrived.at[here],
                       along(p, (first[p] + d) % 4)))
        start(copy(out.at[here], out.at[here], gather_core.at[p, 0, 0], arrived.at[here], partner))

    def received(piece):
        copy(out.at[piece], out.at[piece], gather_core.at[0, 0, 0], arrived.at[piece], partner).wait_recv()

    for e in (1, 3, 2):
        for p in (0, 1):
            piece = (core, p, first[p], (second[p] + e) % 4)
            received(piece)
            for d in (2, 1, 3):
                start(copy(out.at[piece], out.at[piece], gather_first.at[p, e, d - 1], arrived.at[piece],
                           along(p, (first[p] + d) % 4)))
            start(copy(out.at[piece], out.at[piece], gather_core.at[p, 0, e], arrived.at[piece], partner))

    for e in (0, 1, 3, 2):
        for d in (1, 3, 2):
            for p in (0, 1):
                piece = (core, p, (first[p] + d) % 4, (second[p] + e) % 4)
                received(piece)
                start(copy(out.at[piece], out.at[piece], gather_core.at[p, d, e], arrived.at[piece], partner))

    for d in range(4):
        for e in range(4):
            for p in (0, 1):
                received((1 - core, p, (first[p] + d) % 4, (second[p] + e) % 4))
    for c in sent:
        c.wait_send()


def gram_sum(modes, batch):
    rows = 8 * len(PAIRS)
    blocks = len(PAIRS)
    f32, b16 = jnp.float32, jnp.bfloat16
    dma = pltpu.SemaphoreType.DMA
    return pl.pallas_call(
        sum_kernel,
        in_specs=[pl.BlockSpec(memory_space=pltpu.VMEM)] * 2,
        out_specs=pl.BlockSpec(memory_space=pltpu.VMEM),
        out_shape=jax.ShapeDtypeStruct((2, 2, 4, 4, rows, 128), f32),
        scratch_shapes=[
            pltpu.VMEM((2, 3, modes.shape[0], 256), b16),
            pltpu.VMEM((3, 512, modes.shape[0]), b16),
            pltpu.VMEM((blocks, 2, 2, 4, 4, 8, 128), f32),
            pltpu.VMEM((blocks, 2, 4, 4, 8, 128), f32),
            pltpu.VMEM((2, 4, blocks, 4, 8, 128), f32),
            pltpu.VMEM((2, 3, blocks, 4, 8, 128), f32),
            pltpu.VMEM((2, 4, rows, 128), f32),
            pltpu.VMEM((2, 3, rows, 128), f32),
            pltpu.VMEM((2, rows, 128), f32),
            pltpu.VMEM((2, 2, rows, 128), f32),
            pltpu.VMEM((2, rows, 128), f32),
            pltpu.VMEM((2, rows, 128), f32),
            pltpu.VMEM((2, 2, rows, 128), f32),
            dma((blocks,)), dma((blocks,)), dma((len(GROUPS), 2, 3)), dma((len(GROUPS), 2, 3)), dma((2, 3)), dma((2, 3)),
            dma((2,)), dma((2,)), dma((2, 2)), dma((2, 2)),
            dma((2, 3)), dma((2, 4, 3)), dma((2, 4, 4)), dma((2, 2, 4, 4)),
        ],
        compiler_params=pltpu.CompilerParams(
            collective_id=0, has_side_effects=True, vmem_limit_bytes=36 * 2**20),
        name="gram_sum",
    )(modes, batch)


def exact_dot(a, b, dims=((1,), (0,))):
    (a_high, a_low), (b_high, b_low) = split(a), split(b)

    def dot(left, right):
        return lax.dot_general(left, right, (dims, ((), ())), preferred_element_type=jnp.float32)

    return dot(a_high, b_high) + (dot(a_low, b_high) + dot(a_high, b_low))


def lanes(value, index):
    return jnp.broadcast_to(value[:, index:index + 1], value.shape)

def row_of(value, index):
    return jnp.broadcast_to(value[index:index + 1, :], value.shape)

def eliminate(tiles, offset):
    shape = tiles[0].shape
    sub = lax.broadcasted_iota(jnp.int32, shape, 0)
    scales = []
    for g in range(len(tiles)):
        w = tiles[g]
        c = [lanes(w, offset + 8 * g + j) for j in range(8)]
        rows, inv, s = [], [], {}
        pivots = jnp.ones(shape, jnp.float32)
        for j in range(8):
            row = row_of(w, j)
            pivot = row_of(c[j], j)
            r = 1.0 / pivot
            pivots = jnp.where(sub == j, pivot, pivots)
            m = jnp.where(sub > j, c[j] * r, 0.0)
            w = w - m * row
            for k in range(j + 1, 8):
                s[j, k] = row_of(c[k], j)
                c[k] = c[k] - m * s[j, k]
            rows.append(row)
            inv.append(r)
        tiles[g] = w
        scales.append(lax.rsqrt(pivots))
        for h in range(g + 1, len(tiles)):
            v = tiles[h]
            c = [lanes(v, offset + 8 * g + j) for j in range(8)]
            for j in range(8):
                m = c[j] * inv[j]
                v = v - m * rows[j]
                for k in range(j + 1, 8):
                    c[k] = c[k] - m * s[j, k]
            tiles[h] = v
    return [t * q for t, q in zip(tiles, scales)]


def factor(aug):
    n = aug.shape[0]
    for d in range(n // BLOCK):
        o = BLOCK * d
        tile = o // 128 * 128
        odd = d % 2
        block = aug[o:o + BLOCK, tile:tile + 128]
        lane = lax.broadcasted_iota(jnp.int32, (BLOCK, 128), 1)
        row = lax.broadcasted_iota(jnp.int32, (BLOCK, 128), 0)
        eye = jnp.where(lane == row + (0 if odd else 64), 1.0, 0.0)
        w = jnp.where((lane >= 64) if odd else (lane < 64), block, eye)
        tiles = eliminate([w[8 * g:8 * g + 8] for g in range(BLOCK // 8)], 64 if odd else 0)
        w = jnp.concatenate(tiles, axis=0)
        if not odd:
            w = pltpu.roll(w, 64, 1)
        z = w[:, :64]
        new = exact_dot(z, aug[o:o + BLOCK, :])
        aug[o:o + BLOCK, :] = new
        if o + BLOCK < n:
            rest = new[:, :n]
            upd = exact_dot(rest, new, ((0,), (0,)))
            aug[o + BLOCK:, :] = aug[o + BLOCK:, :] - upd[o + BLOCK:, :]

def update_kernel(total_rows, sums_ref, core_ref, modes_ref, batch_ref, out_ref, aug, high, low):
    width = modes_ref.shape[1]
    n = batch_ref.shape[1]

    @pl.when(pl.program_id(0) == 0)
    def _():
        def block(index):
            panels = [sums_ref[h, :, :, :, 8 * index:8 * (index + 1), :].reshape(n, n // 2) for h in range(2)]
            return jnp.concatenate(panels, axis=1)

        first, second = block(3), block(4)
        coeffs = (first * (1.0 / total_rows), second * (1.0 / total_rows))
        mixed = block(1)
        product_first = exact_dot(block(0), coeffs[0]) + exact_dot(mixed, coeffs[1])
        product_second = exact_dot(mixed, coeffs[0], ((0,), (0,))) + exact_dot(block(2), coeffs[1])
        gram = block(5) - exact_dot(coeffs[0], 2.0 * first - product_first, ((0,), (0,)))
        gram = gram - exact_dot(coeffs[1], 2.0 * second - product_second, ((0,), (0,)))
        aug[:, :n] = gram * (1.0 / total_rows)
        row = lax.broadcasted_iota(jnp.int32, (n, n), 0)
        column = lax.broadcasted_iota(jnp.int32, (n, n), 1)
        aug[:, n:] = jnp.where(row == column, 1.0, 0.0)
        factor(aug)
        weights = exact_dot(aug[:, n:], core_ref[width:, :], ((0,), (0,)))
        high[width:, :], low[width:, :] = split(weights)
        for i in range(width // n):
            top = core_ref[n * i:n * (i + 1), :] - exact_dot(coeffs[i], weights)
            high[n * i:n * (i + 1), :], low[n * i:n * (i + 1), :] = split(top)

    values = [split(value) for value in (modes_ref[:, :n], modes_ref[:, n:], batch_ref[...])]
    stacked = jnp.concatenate(
        [jnp.concatenate([v[half] for v in values], axis=1) for half in (0, 1)], axis=0)
    rows = out_ref.shape[0]
    for i in range(width // n):
        columns = slice(n * i, n * (i + 1))
        both = jnp.dot(stacked, high[:, columns], preferred_element_type=jnp.float32)
        other = jnp.dot(stacked[:rows], low[:, columns], preferred_element_type=jnp.float32)
        out_ref[:, columns] = both[:rows] + (both[rows:] + other)


def update(sums, core, modes, batch, total_rows, tile=512):
    rows, width = modes.shape
    n = batch.shape[1]
    return pl.pallas_call(
        functools.partial(update_kernel, total_rows),
        grid=(rows // tile,),
        in_specs=[
            pl.BlockSpec(sums.shape, lambda i: (0,) * 6, pipeline_mode=pl.Buffered(1)),
            pl.BlockSpec(core.shape, lambda i: (0, 0), pipeline_mode=pl.Buffered(1)),
            pl.BlockSpec((tile, width), lambda i: (i, 0)),
            pl.BlockSpec((tile, n), lambda i: (i, 0)),
        ],
        out_specs=pl.BlockSpec((tile, width), lambda i: (i, 0)),
        out_shape=jax.ShapeDtypeStruct((rows, width), jnp.float32),
        scratch_shapes=[
            pltpu.VMEM((n, 2 * n), jnp.float32),
            pltpu.VMEM(core.shape, jnp.bfloat16),
            pltpu.VMEM(core.shape, jnp.bfloat16),
        ],
        compiler_params=pltpu.CompilerParams(
            dimension_semantics=("arbitrary",), vmem_limit_bytes=24 * 2**20),
        name="update",
    )(sums, core, modes, batch)


def shards(modes, batch, core):
    total_rows = modes.shape[0] * lax.axis_size("gx") * lax.axis_size("gy")
    return update(gram_sum(modes, batch), core, modes, batch, total_rows)


def solution(mesh):
    placed = (P(("gx", "gy"), None), P(("gx", "gy"), None), P())
    return jax.shard_map(
        shards, mesh=mesh, in_specs=placed, out_specs=P(("gx", "gy"), None), check_vma=False
    )
```

```python
import functools

import jax
import jax.numpy as jnp
from jax import lax
from jax.experimental import pallas as pl
from jax.experimental.pallas import tpu as pltpu
from jax.sharding import PartitionSpec as P

MESH = pl.DeviceIdType.MESH
NZ, NY, NX = 8, 4, 4
PAIRS = ((0, 0), (0, 1), (1, 1), (0, 2), (1, 2), (2, 2))
BLOCK = 64
GROUPS = ((0, 3), (3, 6))


def split(value):
    high = value.astype(jnp.bfloat16)
    low = (value - high.astype(jnp.float32)).astype(jnp.bfloat16)
    return high, low


LOADS = 2


def loads(modes, batch, raw, load_sem):
    step = raw.shape[1] // LOADS
    copies = []
    for g in range(3):
        for i in range(LOADS):
            here = pl.ds(i * step, step)
            source = modes.at[here, pl.ds(256 * g, 256)] if g < 2 else batch.at[here]
            copies.append(pltpu.make_async_copy(source, raw.at[g, here], load_sem.at[g, i]))
    return copies


def split_group(g, copies, raw, parts, flipped):
    rows = raw.shape[1]
    step = rows // LOADS
    for i in range(LOADS):
        copies[LOADS * g + i].wait()
        here = pl.ds(i * step, step)
        high, low = split(raw[g, here])
        parts[0, g, here] = high
        parts[1, g, here] = low
        flipped[g, :256, here] = high.T
        flipped[g, 256:, here] = low.T


def gram_block(i, j, parts, flipped):
    both = jnp.dot(flipped[i], parts[0, j], preferred_element_type=jnp.float32)
    mixed = both[256:]
    if i == j:
        return both[:256] + (mixed + mixed.T)
    other = jnp.dot(flipped[i, :256], parts[1, j], preferred_element_type=jnp.float32)
    return both[:256] + (mixed + other)


def sum_kernel(
    modes, batch, out, parts, raw, load_sem, flipped,
    part, from_core, half, from_first, quarter, from_second, mine, from_near, three, pair, from_far,
    core_send, core_recv, first_send, first_recv, second_send, second_recv, near_send, near_recv, far_send, far_recv,
    gather_second, gather_first, gather_core, arrived,
):
    gx, gy = lax.axis_index("gx"), lax.axis_index("gy")
    z, core = gx // 2, gx % 2
    y, x = gy // NX, gy % NX
    partner = (z * 2 + (1 - core), gy)
    first, second = (x, y), (y, x)

    def along(axis, index):
        return (gx, y * NX + index) if axis == 0 else (gx, index * NX + x)

    def at_z(index):
        return (index * 2 + core, gy)

    def copy(src, dst, send, recv, device):
        return pltpu.make_async_remote_copy(
            src_ref=src, dst_ref=dst, send_sem=send, recv_sem=recv,
            device_id=device, device_id_type=MESH,
        )

    copies = loads(modes, batch, raw, load_sem)
    for c in copies:
        c.start()
    barrier = pltpu.get_barrier_semaphore()
    peers = [partner]
    peers += [along(0, (x + d) % NX) for d in range(1, NX)]
    peers += [along(1, (y + d) % NY) for d in range(1, NY)]
    peers += [at_z((z + d) % NZ) for d in (1, 2, 3, 5, 6, 7)]
    for peer in peers:
        pl.semaphore_signal(barrier, inc=1, device_id=peer, device_id_type=MESH)

    sent = []

    def start(c):
        c.start()
        sent.append(c)
        return c

    first_copies = {}

    def keep_half(t, core_copy):
        core_copy.wait_recv()
        kept = part[t, core] + from_core[t]
        for p in (0, 1):
            for a in range(4):
                half[p, a, t] = kept[p, a]

    def along_first(group):
        begin, end = GROUPS[group]
        for d in (2, 1, 3):
            for p in (0, 1):
                a = (first[p] + d) % 4
                first_copies[group, p, d] = start(copy(
                    half.at[p, a, pl.ds(begin, end - begin)], from_first.at[p, d - 1, pl.ds(begin, end - begin)],
                    first_send.at[group, p, d - 1], first_recv.at[group, p, d - 1], along(p, a)))

    split_group(0, copies, raw, parts, flipped)
    pending = None
    for t, (i, j) in enumerate(PAIRS):
        if t < 2:
            split_group(t + 1, copies, raw, parts, flipped)
        block = gram_block(i, j, parts, flipped)
        for h in range(2):
            part[t, h] = block[:, 128 * h:128 * (h + 1)].reshape(2, 4, 4, 8, 128)
        if t == 0:
            pl.semaphore_wait(barrier, len(peers))
        core_copy = start(copy(
            part.at[t, 1 - core], from_core.at[t], core_send.at[t], core_recv.at[t], partner))
        if pending is not None:
            keep_half(t - 1, pending)
            for group, (begin, end) in enumerate(GROUPS):
                if end == t:
                    along_first(group)
        pending = core_copy
    keep_half(len(PAIRS) - 1, pending)
    along_first(len(GROUPS) - 1)

    second_copies = {}
    for p in (0, 1):
        for group in range(len(GROUPS)):
            for d in (2, 1, 3):
                first_copies[group, p, d].wait_recv()
        for d in (2, 1, 3, 0):
            b = (second[p] + d) % 4
            for t in range(len(PAIRS)):
                quarter[p, d, 8 * t:8 * (t + 1)] = (half[p, first[p], t, b] + from_first[p, 0, t, b]) + (
                    from_first[p, 1, t, b] + from_first[p, 2, t, b])
            if d:
                second_copies[p, d] = start(copy(
                    quarter.at[p, d], from_second.at[p, d - 1], second_send.at[p, d - 1],
                    second_recv.at[p, d - 1], along(1 - p, b)))

    for p in (0, 1):
        for d in (2, 1, 3):
            second_copies[p, d].wait_recv()
        mine[p] = (quarter[p, 0] + from_second[p, 0]) + (from_second[p, 1] + from_second[p, 2])

    z_copies = {}
    for side in (0, 1):
        z_copies[side] = start(copy(
            mine, from_near.at[side], near_send.at[side], near_recv.at[side], at_z((z + (1, 7)[side]) % NZ)))
    for side in (0, 1):
        z_copies[side].wait_recv()
    far_copies = []
    for p in (0, 1):
        two = mine[p] + from_near[1 - p, p]
        pair[p] = two
        three[p] = two + from_near[p, p]
        far_copies.append(start(copy(
            three.at[p], from_far.at[p, 0], far_send.at[p, 0], far_recv.at[p, 0], at_z((z + (3, 5)[p]) % NZ))))
        far_copies.append(start(copy(
            pair.at[p], from_far.at[p, 1], far_send.at[p, 1], far_recv.at[p, 1], at_z((z + (6, 2)[p]) % NZ))))
    for c in far_copies:
        c.wait_recv()

    for p in (0, 1):
        here = (core, p, first[p], second[p])
        out[here] = three[p] + (from_far[p, 0] + from_far[p, 1])
        for d in (2, 1, 3):
            start(copy(out.at[here], out.at[here], gather_second.at[p, d - 1], arrived.at[here],
                       along(1 - p, (second[p] + d) % 4)))
        for d in (2, 1, 3):
            start(copy(out.at[here], out.at[here], gather_first.at[p, 0, d - 1], arrived.at[here],
                       along(p, (first[p] + d) % 4)))
        start(copy(out.at[here], out.at[here], gather_core.at[p, 0, 0], arrived.at[here], partner))

    def received(piece):
        copy(out.at[piece], out.at[piece], gather_core.at[0, 0, 0], arrived.at[piece], partner).wait_recv()

    for e in (1, 3, 2):
        for p in (0, 1):
            piece = (core, p, first[p], (second[p] + e) % 4)
            received(piece)
            for d in (2, 1, 3):
                start(copy(out.at[piece], out.at[piece], gather_first.at[p, e, d - 1], arrived.at[piece],
                           along(p, (first[p] + d) % 4)))
            start(copy(out.at[piece], out.at[piece], gather_core.at[p, 0, e], arrived.at[piece], partner))

    for e in (0, 1, 3, 2):
        for d in (1, 3, 2):
            for p in (0, 1):
                piece = (core, p, (first[p] + d) % 4, (second[p] + e) % 4)
                received(piece)
                start(copy(out.at[piece], out.at[piece], gather_core.at[p, d, e], arrived.at[piece], partner))

    for d in range(4):
        for e in range(4):
            for p in (0, 1):
                received((1 - core, p, (first[p] + d) % 4, (second[p] + e) % 4))
    for c in sent:
        c.wait_send()


def gram_sum(modes, batch):
    rows = 8 * len(PAIRS)
    blocks = len(PAIRS)
    f32, b16 = jnp.float32, jnp.bfloat16
    dma = pltpu.SemaphoreType.DMA
    return pl.pallas_call(
        sum_kernel,
        in_specs=[pl.BlockSpec(memory_space=pltpu.HBM)] * 2,
        out_specs=[pl.BlockSpec(memory_space=pltpu.VMEM)] * 2,
        out_shape=[
            jax.ShapeDtypeStruct((2, 2, 4, 4, rows, 128), f32),
            jax.ShapeDtypeStruct((2, 3, modes.shape[0], 256), b16),
        ],
        scratch_shapes=[
            pltpu.VMEM((3, modes.shape[0], 256), f32),
            dma((3, LOADS)),
            pltpu.VMEM((3, 512, modes.shape[0]), b16),
            pltpu.VMEM((blocks, 2, 2, 4, 4, 8, 128), f32),
            pltpu.VMEM((blocks, 2, 4, 4, 8, 128), f32),
            pltpu.VMEM((2, 4, blocks, 4, 8, 128), f32),
            pltpu.VMEM((2, 3, blocks, 4, 8, 128), f32),
            pltpu.VMEM((2, 4, rows, 128), f32),
            pltpu.VMEM((2, 3, rows, 128), f32),
            pltpu.VMEM((2, rows, 128), f32),
            pltpu.VMEM((2, 2, rows, 128), f32),
            pltpu.VMEM((2, rows, 128), f32),
            pltpu.VMEM((2, rows, 128), f32),
            pltpu.VMEM((2, 2, rows, 128), f32),
            dma((blocks,)), dma((blocks,)), dma((len(GROUPS), 2, 3)), dma((len(GROUPS), 2, 3)), dma((2, 3)), dma((2, 3)),
            dma((2,)), dma((2,)), dma((2, 2)), dma((2, 2)),
            dma((2, 3)), dma((2, 4, 3)), dma((2, 4, 4)), dma((2, 2, 4, 4)),
        ],
        compiler_params=pltpu.CompilerParams(
            collective_id=0, has_side_effects=True, vmem_limit_bytes=36 * 2**20),
        name="gram_sum",
    )(modes, batch)


def exact_dot(a, b, dims=((1,), (0,))):
    (a_high, a_low), (b_high, b_low) = split(a), split(b)

    def dot(left, right):
        return lax.dot_general(left, right, (dims, ((), ())), preferred_element_type=jnp.float32)

    return dot(a_high, b_high) + (dot(a_low, b_high) + dot(a_high, b_low))


def lanes(value, index):
    return jnp.broadcast_to(value[:, index:index + 1], value.shape)

def row_of(value, index):
    return jnp.broadcast_to(value[index:index + 1, :], value.shape)

def eliminate(tiles, offset):
    shape = tiles[0].shape
    sub = lax.broadcasted_iota(jnp.int32, shape, 0)
    scales = []
    for g in range(len(tiles)):
        w = tiles[g]
        c = [lanes(w, offset + 8 * g + j) for j in range(8)]
        rows, inv, s = [], [], {}
        pivots = jnp.ones(shape, jnp.float32)
        for j in range(8):
            row = row_of(w, j)
            pivot = row_of(c[j], j)
            r = 1.0 / pivot
            pivots = jnp.where(sub == j, pivot, pivots)
            m = jnp.where(sub > j, c[j] * r, 0.0)
            w = w - m * row
            for k in range(j + 1, 8):
                s[j, k] = row_of(c[k], j)
                c[k] = c[k] - m * s[j, k]
            rows.append(row)
            inv.append(r)
        tiles[g] = w
        scales.append(lax.rsqrt(pivots))
        for h in range(g + 1, len(tiles)):
            v = tiles[h]
            c = [lanes(v, offset + 8 * g + j) for j in range(8)]
            for j in range(8):
                m = c[j] * inv[j]
                v = v - m * rows[j]
                for k in range(j + 1, 8):
                    c[k] = c[k] - m * s[j, k]
            tiles[h] = v
    return [t * q for t, q in zip(tiles, scales)]


def factor(aug):
    n = aug.shape[0]
    for d in range(n // BLOCK):
        o = BLOCK * d
        tile = o // 128 * 128
        odd = d % 2
        block = aug[o:o + BLOCK, tile:tile + 128]
        lane = lax.broadcasted_iota(jnp.int32, (BLOCK, 128), 1)
        row = lax.broadcasted_iota(jnp.int32, (BLOCK, 128), 0)
        eye = jnp.where(lane == row + (0 if odd else 64), 1.0, 0.0)
        w = jnp.where((lane >= 64) if odd else (lane < 64), block, eye)
        tiles = eliminate([w[8 * g:8 * g + 8] for g in range(BLOCK // 8)], 64 if odd else 0)
        w = jnp.concatenate(tiles, axis=0)
        if not odd:
            w = pltpu.roll(w, 64, 1)
        z = w[:, :64]
        new = exact_dot(z, aug[o:o + BLOCK, :])
        aug[o:o + BLOCK, :] = new
        if o + BLOCK < n:
            rest = new[:, :n]
            upd = exact_dot(rest, new, ((0,), (0,)))
            aug[o + BLOCK:, :] = aug[o + BLOCK:, :] - upd[o + BLOCK:, :]

def update_kernel(total_rows, sums_ref, core_ref, parts_ref, out_ref, aug, high, low):
    width = core_ref.shape[1]
    n = core_ref.shape[0] - width

    @pl.when(pl.program_id(0) == 0)
    def _():
        def block(index):
            panels = [sums_ref[h, :, :, :, 8 * index:8 * (index + 1), :].reshape(n, n // 2) for h in range(2)]
            return jnp.concatenate(panels, axis=1)

        first, second = block(3), block(4)
        coeffs = (first * (1.0 / total_rows), second * (1.0 / total_rows))
        mixed = block(1)
        product_first = exact_dot(block(0), coeffs[0]) + exact_dot(mixed, coeffs[1])
        product_second = exact_dot(mixed, coeffs[0], ((0,), (0,))) + exact_dot(block(2), coeffs[1])
        gram = block(5) - exact_dot(coeffs[0], 2.0 * first - product_first, ((0,), (0,)))
        gram = gram - exact_dot(coeffs[1], 2.0 * second - product_second, ((0,), (0,)))
        aug[:, :n] = gram * (1.0 / total_rows)
        row = lax.broadcasted_iota(jnp.int32, (n, n), 0)
        column = lax.broadcasted_iota(jnp.int32, (n, n), 1)
        aug[:, n:] = jnp.where(row == column, 1.0, 0.0)
        factor(aug)
        weights = exact_dot(aug[:, n:], core_ref[width:, :], ((0,), (0,)))
        high[width:, :], low[width:, :] = split(weights)
        for i in range(width // n):
            top = core_ref[n * i:n * (i + 1), :] - exact_dot(coeffs[i], weights)
            high[n * i:n * (i + 1), :], low[n * i:n * (i + 1), :] = split(top)

    stacked = jnp.concatenate(
        [jnp.concatenate([parts_ref[half, g] for g in range(3)], axis=1) for half in (0, 1)], axis=0)
    rows = out_ref.shape[0]
    for i in range(width // n):
        columns = slice(n * i, n * (i + 1))
        both = jnp.dot(stacked, high[:, columns], preferred_element_type=jnp.float32)
        other = jnp.dot(stacked[:rows], low[:, columns], preferred_element_type=jnp.float32)
        out_ref[:, columns] = both[:rows] + (both[rows:] + other)


def update(sums, core, parts, total_rows, tile=512):
    rows, width = parts.shape[2], core.shape[1]
    n = core.shape[0] - width
    return pl.pallas_call(
        functools.partial(update_kernel, total_rows),
        grid=(rows // tile,),
        in_specs=[
            pl.BlockSpec(sums.shape, lambda i: (0,) * 6, pipeline_mode=pl.Buffered(1)),
            pl.BlockSpec(core.shape, lambda i: (0, 0), pipeline_mode=pl.Buffered(1)),
            pl.BlockSpec((2, 3, tile, 256), lambda i: (0, 0, i, 0)),
        ],
        out_specs=pl.BlockSpec((tile, width), lambda i: (i, 0)),
        out_shape=jax.ShapeDtypeStruct((rows, width), jnp.float32),
        scratch_shapes=[
            pltpu.VMEM((n, 2 * n), jnp.float32),
            pltpu.VMEM(core.shape, jnp.bfloat16),
            pltpu.VMEM(core.shape, jnp.bfloat16),
        ],
        compiler_params=pltpu.CompilerParams(
            dimension_semantics=("arbitrary",), vmem_limit_bytes=24 * 2**20),
        name="update",
    )(sums, core, parts)


def shards(modes, batch, core):
    total_rows = modes.shape[0] * lax.axis_size("gx") * lax.axis_size("gy")
    modes = pltpu.with_memory_space_constraint(modes, pltpu.HBM)
    batch = pltpu.with_memory_space_constraint(batch, pltpu.HBM)
    sums, parts = gram_sum(modes, batch)
    return update(sums, core, parts, total_rows)


def solution(mesh):
    placed = (P(("gx", "gy"), None), P(("gx", "gy"), None), P())
    return jax.shard_map(
        shards, mesh=mesh, in_specs=placed, out_specs=P(("gx", "gy"), None), check_vma=False
    )
```

```python
import functools

import jax
import jax.numpy as jnp
from jax import lax
from jax.experimental import pallas as pl
from jax.experimental.pallas import tpu as pltpu
from jax.sharding import PartitionSpec as P

MESH = pl.DeviceIdType.MESH
NZ, NY, NX = 8, 4, 4
PAIRS = ((0, 0), (0, 1), (1, 1), (0, 2), (1, 2), (2, 2))
BLOCK = 64
GROUPS = ((0, 4), (4, 6))


def split(value):
    high = value.astype(jnp.bfloat16)
    low = (value - high.astype(jnp.float32)).astype(jnp.bfloat16)
    return high, low


LOADS = 2


def loads(modes, batch, raw, load_sem):
    step = raw.shape[1] // LOADS
    copies = []
    for g in range(3):
        for i in range(LOADS):
            here = pl.ds(i * step, step)
            source = modes.at[here, pl.ds(256 * g, 256)] if g < 2 else batch.at[here]
            copies.append(pltpu.make_async_copy(source, raw.at[g, here], load_sem.at[g, i]))
    return copies


def split_group(g, copies, raw, parts, flipped):
    rows = raw.shape[1]
    step = rows // LOADS
    for i in range(LOADS):
        copies[LOADS * g + i].wait()
        here = pl.ds(i * step, step)
        high, low = split(raw[g, here])
        parts[0, g, here] = high
        parts[1, g, here] = low
        flipped[g, :256, here] = high.T
        flipped[g, 256:, here] = low.T


def gram_block(i, j, parts, flipped):
    both = jnp.dot(flipped[i], parts[0, j], preferred_element_type=jnp.float32)
    mixed = both[256:]
    if i == j:
        return both[:256] + (mixed + mixed.T)
    other = jnp.dot(flipped[i, :256], parts[1, j], preferred_element_type=jnp.float32)
    return both[:256] + (mixed + other)


def sum_kernel(
    modes, batch, out, parts, raw, load_sem, flipped,
    part, from_core, half, from_first, quarter, from_second, mine, from_near, three, pair, from_far,
    core_send, core_recv, first_send, first_recv, second_send, second_recv, near_send, near_recv, far_send, far_recv,
    gather_second, gather_first, gather_core, arrived,
):
    gx, gy = lax.axis_index("gx"), lax.axis_index("gy")
    z, core = gx // 2, gx % 2
    y, x = gy // NX, gy % NX
    partner = (z * 2 + (1 - core), gy)
    first, second = (x, y), (y, x)

    def along(axis, index):
        return (gx, y * NX + index) if axis == 0 else (gx, index * NX + x)

    def at_z(index):
        return (index * 2 + core, gy)

    def copy(src, dst, send, recv, device):
        return pltpu.make_async_remote_copy(
            src_ref=src, dst_ref=dst, send_sem=send, recv_sem=recv,
            device_id=device, device_id_type=MESH,
        )

    copies = loads(modes, batch, raw, load_sem)
    for c in copies:
        c.start()
    barrier = pltpu.get_barrier_semaphore()
    peers = [partner]
    peers += [along(0, (x + d) % NX) for d in range(1, NX)]
    peers += [along(1, (y + d) % NY) for d in range(1, NY)]
    peers += [at_z((z + d) % NZ) for d in (1, 2, 3, 5, 6, 7)]
    for peer in peers:
        pl.semaphore_signal(barrier, inc=1, device_id=peer, device_id_type=MESH)

    sent = []

    def start(c):
        c.start()
        sent.append(c)
        return c

    first_copies = {}

    def keep_half(t, core_copy):
        core_copy.wait_recv()
        kept = part[t, core] + from_core[t]
        for p in (0, 1):
            for a in range(4):
                half[p, a, t] = kept[p, a]

    def along_first(group):
        begin, end = GROUPS[group]
        for d in (2, 1, 3):
            for p in (0, 1):
                a = (first[p] + d) % 4
                first_copies[group, p, d] = start(copy(
                    half.at[p, a, pl.ds(begin, end - begin)], from_first.at[p, d - 1, pl.ds(begin, end - begin)],
                    first_send.at[group, p, d - 1], first_recv.at[group, p, d - 1], along(p, a)))

    split_group(0, copies, raw, parts, flipped)
    pending = None
    for t, (i, j) in enumerate(PAIRS):
        if t < 2:
            split_group(t + 1, copies, raw, parts, flipped)
        block = gram_block(i, j, parts, flipped)
        for h in range(2):
            part[t, h] = block[:, 128 * h:128 * (h + 1)].reshape(2, 4, 4, 8, 128)
        if t == 0:
            pl.semaphore_wait(barrier, len(peers))
        core_copy = start(copy(
            part.at[t, 1 - core], from_core.at[t], core_send.at[t], core_recv.at[t], partner))
        if pending is not None:
            keep_half(t - 1, pending)
            for group, (begin, end) in enumerate(GROUPS):
                if end == t:
                    along_first(group)
        pending = core_copy
    keep_half(len(PAIRS) - 1, pending)
    along_first(len(GROUPS) - 1)

    second_copies = {}
    for p in (0, 1):
        for group in range(len(GROUPS)):
            for d in (2, 1, 3):
                first_copies[group, p, d].wait_recv()
        for d in (2, 1, 3, 0):
            b = (second[p] + d) % 4
            for t in range(len(PAIRS)):
                quarter[p, d, 8 * t:8 * (t + 1)] = (half[p, first[p], t, b] + from_first[p, 0, t, b]) + (
                    from_first[p, 1, t, b] + from_first[p, 2, t, b])
            if d:
                second_copies[p, d] = start(copy(
                    quarter.at[p, d], from_second.at[p, d - 1], second_send.at[p, d - 1],
                    second_recv.at[p, d - 1], along(1 - p, b)))

    for p in (0, 1):
        for d in (2, 1, 3):
            second_copies[p, d].wait_recv()
        mine[p] = (quarter[p, 0] + from_second[p, 0]) + (from_second[p, 1] + from_second[p, 2])

    z_copies = {}
    for side in (0, 1):
        z_copies[side] = start(copy(
            mine, from_near.at[side], near_send.at[side], near_recv.at[side], at_z((z + (1, 7)[side]) % NZ)))
    for side in (0, 1):
        z_copies[side].wait_recv()
    far_copies = []
    for p in (0, 1):
        two = mine[p] + from_near[1 - p, p]
        pair[p] = two
        three[p] = two + from_near[p, p]
        far_copies.append(start(copy(
            three.at[p], from_far.at[p, 0], far_send.at[p, 0], far_recv.at[p, 0], at_z((z + (3, 5)[p]) % NZ))))
        far_copies.append(start(copy(
            pair.at[p], from_far.at[p, 1], far_send.at[p, 1], far_recv.at[p, 1], at_z((z + (6, 2)[p]) % NZ))))
    for c in far_copies:
        c.wait_recv()

    for p in (0, 1):
        here = (core, p, first[p], second[p])
        out[here] = three[p] + (from_far[p, 0] + from_far[p, 1])
        for d in (2, 1, 3):
            start(copy(out.at[here], out.at[here], gather_second.at[p, d - 1], arrived.at[here],
                       along(1 - p, (second[p] + d) % 4)))
        for d in (2, 1, 3):
            start(copy(out.at[here], out.at[here], gather_first.at[p, 0, d - 1], arrived.at[here],
                       along(p, (first[p] + d) % 4)))
        start(copy(out.at[here], out.at[here], gather_core.at[p, 0, 0], arrived.at[here], partner))

    def received(piece):
        copy(out.at[piece], out.at[piece], gather_core.at[0, 0, 0], arrived.at[piece], partner).wait_recv()

    for e in (1, 3, 2):
        for p in (0, 1):
            piece = (core, p, first[p], (second[p] + e) % 4)
            received(piece)
            for d in (2, 1, 3):
                start(copy(out.at[piece], out.at[piece], gather_first.at[p, e, d - 1], arrived.at[piece],
                           along(p, (first[p] + d) % 4)))
            start(copy(out.at[piece], out.at[piece], gather_core.at[p, 0, e], arrived.at[piece], partner))

    for e in (0, 1, 3, 2):
        for d in (1, 3, 2):
            for p in (0, 1):
                piece = (core, p, (first[p] + d) % 4, (second[p] + e) % 4)
                received(piece)
                start(copy(out.at[piece], out.at[piece], gather_core.at[p, d, e], arrived.at[piece], partner))

    for d in range(4):
        for e in range(4):
            for p in (0, 1):
                received((1 - core, p, (first[p] + d) % 4, (second[p] + e) % 4))
    for c in sent:
        c.wait_send()


def gram_sum(modes, batch):
    rows = 8 * len(PAIRS)
    blocks = len(PAIRS)
    f32, b16 = jnp.float32, jnp.bfloat16
    dma = pltpu.SemaphoreType.DMA
    return pl.pallas_call(
        sum_kernel,
        in_specs=[pl.BlockSpec(memory_space=pltpu.HBM)] * 2,
        out_specs=[pl.BlockSpec(memory_space=pltpu.VMEM)] * 2,
        out_shape=[
            jax.ShapeDtypeStruct((2, 2, 4, 4, rows, 128), f32),
            jax.ShapeDtypeStruct((2, 3, modes.shape[0], 256), b16),
        ],
        scratch_shapes=[
            pltpu.VMEM((3, modes.shape[0], 256), f32),
            dma((3, LOADS)),
            pltpu.VMEM((3, 512, modes.shape[0]), b16),
            pltpu.VMEM((blocks, 2, 2, 4, 4, 8, 128), f32),
            pltpu.VMEM((blocks, 2, 4, 4, 8, 128), f32),
            pltpu.VMEM((2, 4, blocks, 4, 8, 128), f32),
            pltpu.VMEM((2, 3, blocks, 4, 8, 128), f32),
            pltpu.VMEM((2, 4, rows, 128), f32),
            pltpu.VMEM((2, 3, rows, 128), f32),
            pltpu.VMEM((2, rows, 128), f32),
            pltpu.VMEM((2, 2, rows, 128), f32),
            pltpu.VMEM((2, rows, 128), f32),
            pltpu.VMEM((2, rows, 128), f32),
            pltpu.VMEM((2, 2, rows, 128), f32),
            dma((blocks,)), dma((blocks,)), dma((len(GROUPS), 2, 3)), dma((len(GROUPS), 2, 3)), dma((2, 3)), dma((2, 3)),
            dma((2,)), dma((2,)), dma((2, 2)), dma((2, 2)),
            dma((2, 3)), dma((2, 4, 3)), dma((2, 4, 4)), dma((2, 2, 4, 4)),
        ],
        compiler_params=pltpu.CompilerParams(
            collective_id=0, has_side_effects=True, vmem_limit_bytes=36 * 2**20),
        name="gram_sum",
    )(modes, batch)


def exact_dot(a, b, dims=((1,), (0,))):
    (a_high, a_low), (b_high, b_low) = split(a), split(b)

    def dot(left, right):
        return lax.dot_general(left, right, (dims, ((), ())), preferred_element_type=jnp.float32)

    return dot(a_high, b_high) + (dot(a_low, b_high) + dot(a_high, b_low))


def lanes(value, index):
    return jnp.broadcast_to(value[:, index:index + 1], value.shape)

def row_of(value, index):
    return jnp.broadcast_to(value[index:index + 1, :], value.shape)

def eliminate(tiles, offset):
    shape = tiles[0].shape
    sub = lax.broadcasted_iota(jnp.int32, shape, 0)
    scales = []
    for g in range(len(tiles)):
        w = tiles[g]
        c = [lanes(w, offset + 8 * g + j) for j in range(8)]
        rows, inv, s = [], [], {}
        pivots = jnp.ones(shape, jnp.float32)
        for j in range(8):
            row = row_of(w, j)
            pivot = row_of(c[j], j)
            r = 1.0 / pivot
            pivots = jnp.where(sub == j, pivot, pivots)
            m = jnp.where(sub > j, c[j] * r, 0.0)
            w = w - m * row
            for k in range(j + 1, 8):
                s[j, k] = row_of(c[k], j)
                c[k] = c[k] - m * s[j, k]
            rows.append(row)
            inv.append(r)
        tiles[g] = w
        scales.append(lax.rsqrt(pivots))
        for h in range(g + 1, len(tiles)):
            v = tiles[h]
            c = [lanes(v, offset + 8 * g + j) for j in range(8)]
            for j in range(8):
                m = c[j] * inv[j]
                v = v - m * rows[j]
                for k in range(j + 1, 8):
                    c[k] = c[k] - m * s[j, k]
            tiles[h] = v
    return [t * q for t, q in zip(tiles, scales)]


def factor(aug):
    n = aug.shape[0]
    for d in range(n // BLOCK):
        o = BLOCK * d
        tile = o // 128 * 128
        odd = d % 2
        block = aug[o:o + BLOCK, tile:tile + 128]
        lane = lax.broadcasted_iota(jnp.int32, (BLOCK, 128), 1)
        row = lax.broadcasted_iota(jnp.int32, (BLOCK, 128), 0)
        eye = jnp.where(lane == row + (0 if odd else 64), 1.0, 0.0)
        w = jnp.where((lane >= 64) if odd else (lane < 64), block, eye)
        tiles = eliminate([w[8 * g:8 * g + 8] for g in range(BLOCK // 8)], 64 if odd else 0)
        w = jnp.concatenate(tiles, axis=0)
        if not odd:
            w = pltpu.roll(w, 64, 1)
        z = w[:, :64]
        begin = (o + BLOCK) // 128 * 128
        end = n + (o + BLOCK + 127) // 128 * 128
        new = exact_dot(z, aug[o:o + BLOCK, begin:end])
        aug[o:o + BLOCK, begin:end] = new
        if o + BLOCK < n:
            change = exact_dot(new[:, :n - begin], new, ((0,), (0,)))
            aug[o + BLOCK:, begin:end] = aug[o + BLOCK:, begin:end] - change[o + BLOCK - begin:, :]


def update_kernel(total_rows, sums_ref, core_ref, parts_ref, out_ref, aug, high, low):
    width = core_ref.shape[1]
    n = core_ref.shape[0] - width

    @pl.when(pl.program_id(0) == 0)
    def _():
        def block(index):
            panels = [sums_ref[h, :, :, :, 8 * index:8 * (index + 1), :].reshape(n, n // 2) for h in range(2)]
            return jnp.concatenate(panels, axis=1)

        first, second = block(3), block(4)
        coeffs = (first * (1.0 / total_rows), second * (1.0 / total_rows))
        mixed = block(1)
        product_first = exact_dot(block(0), coeffs[0]) + exact_dot(mixed, coeffs[1])
        product_second = exact_dot(mixed, coeffs[0], ((0,), (0,))) + exact_dot(block(2), coeffs[1])
        gram = block(5) - exact_dot(coeffs[0], 2.0 * first - product_first, ((0,), (0,)))
        gram = gram - exact_dot(coeffs[1], 2.0 * second - product_second, ((0,), (0,)))
        aug[:, :n] = gram * (1.0 / total_rows)
        row = lax.broadcasted_iota(jnp.int32, (n, n), 0)
        column = lax.broadcasted_iota(jnp.int32, (n, n), 1)
        aug[:, n:] = jnp.where(row == column, 1.0, 0.0)
        factor(aug)
        weights = exact_dot(aug[:, n:], core_ref[width:, :], ((0,), (0,)))
        high[width:, :], low[width:, :] = split(weights)
        for i in range(width // n):
            top = core_ref[n * i:n * (i + 1), :] - exact_dot(coeffs[i], weights)
            high[n * i:n * (i + 1), :], low[n * i:n * (i + 1), :] = split(top)

    stacked = jnp.concatenate(
        [jnp.concatenate([parts_ref[half, g] for g in range(3)], axis=1) for half in (0, 1)], axis=0)
    rows = out_ref.shape[0]
    for i in range(width // n):
        columns = slice(n * i, n * (i + 1))
        both = jnp.dot(stacked, high[:, columns], preferred_element_type=jnp.float32)
        other = jnp.dot(stacked[:rows], low[:, columns], preferred_element_type=jnp.float32)
        out_ref[:, columns] = both[:rows] + (both[rows:] + other)


def update(sums, core, parts, total_rows, tile=512):
    rows, width = parts.shape[2], core.shape[1]
    n = core.shape[0] - width
    return pl.pallas_call(
        functools.partial(update_kernel, total_rows),
        grid=(rows // tile,),
        in_specs=[
            pl.BlockSpec(sums.shape, lambda i: (0,) * 6, pipeline_mode=pl.Buffered(1)),
            pl.BlockSpec(core.shape, lambda i: (0, 0), pipeline_mode=pl.Buffered(1)),
            pl.BlockSpec((2, 3, tile, 256), lambda i: (0, 0, i, 0)),
        ],
        out_specs=pl.BlockSpec((tile, width), lambda i: (i, 0)),
        out_shape=jax.ShapeDtypeStruct((rows, width), jnp.float32),
        scratch_shapes=[
            pltpu.VMEM((n, 2 * n), jnp.float32),
            pltpu.VMEM(core.shape, jnp.bfloat16),
            pltpu.VMEM(core.shape, jnp.bfloat16),
        ],
        compiler_params=pltpu.CompilerParams(
            dimension_semantics=("arbitrary",), vmem_limit_bytes=24 * 2**20),
        name="update",
    )(sums, core, parts)


def shards(modes, batch, core):
    total_rows = modes.shape[0] * lax.axis_size("gx") * lax.axis_size("gy")
    modes = pltpu.with_memory_space_constraint(modes, pltpu.HBM)
    batch = pltpu.with_memory_space_constraint(batch, pltpu.HBM)
    sums, parts = gram_sum(modes, batch)
    return update(sums, core, parts, total_rows)


def solution(mesh):
    placed = (P(("gx", "gy"), None), P(("gx", "gy"), None), P())
    return jax.shard_map(
        shards, mesh=mesh, in_specs=placed, out_specs=P(("gx", "gy"), None), check_vma=False
    )
```
